32 devices in a mesh: gx: 8 (over z, y), gy: 2 (over x), gz: 2 (over core).
Axes of the slice: x: 2, y: 2, z: 4, core: 2. Of those that a mesh axis runs over, the one named last changes fastest.
Arguments:
- populations: float32 [19, 64, 32, 256], P(None, 'gx', 'gy', 'gz'), as said below
- coarse_pops: float32 [19, 32, 16, 128], P(None, 'gx', 'gy', 'gz'), as said below
- fine_mask: int32 [64, 32, 256], P('gx', 'gy', 'gz'), may hold values 0 or 1
- coarse_mask: int32 [32, 16, 128], P('gx', 'gy', 'gz'), may hold values 0 or 1
- bead_data: float32 [8, 2, 2, 6, 512], P('gx', 'gy', 'gz'), as said below
- bead_bins: int32 [8, 2, 2, 1, 512], P('gx', 'gy', 'gz'), may hold values from -1 to 127, as said below
Outputs:
- fine_out: float32 [19, 64, 32, 256], P(None, 'gx', 'gy', 'gz')
- coarse_out: float32 [19, 32, 16, 128], P(None, 'gx', 'gy', 'gz')
The draws below stay inside these ranges and needn't reach their ends.
Inputs may be any that keep to these rules, and one draw needn't show every extreme that they name: `populations`: populations are positive; rest population near 1/3, axis ones near 1/18, edge ones near 1/36, density within 0.5 to 1.7. `coarse_pops`: same law as populations on the coarse grid. `bead_bins`: in each source's block of 32 slots for one owner, the live slots come first; one owner receives 32 live slots from every source in every draw. `bead_data`: row 0 and 1 lie in -0.5 to 1.5, row 2 in -0.5 to 32 - 0.5; values in empty slots are arbitrary.
All inputs are finite; a program needn't handle non-finite values. No bound on the sum of `fine_mask` or of `coarse_mask` on one device may be relied on, other than what follows from the above.
Results may differ from the reference program's by a relative error of at most 0.0003.
Values sent between devices are 32-bit elements; how exact they have to be, the bound alone decides.
A program may use at most 128 MiB of HBM per device.

```python
import jax
import jax.numpy as jnp
import numpy as np
from jax import lax

Q = 19
BIN_Z = 32
SLOT = 32
NX = 64
NY = 32
NZ = 256
N_GX = 8
N_GY = 2
N_GZ = 2


LATTICE_WEIGHTS = np.array([1.0 / 3.0] + [1.0 / 18.0] * 6 + [1.0 / 36.0] * 12)


def lattice_field(key, shape):
    first, second = jax.random.split(key)
    grid = shape[1:]
    density = 1.0 + 0.15 * jax.random.uniform(first, grid, jnp.float32, -1.0, 1.0)
    noise = 0.4 * jax.random.uniform(second, shape, jnp.float32, -1.0, 1.0)
    weights = jnp.asarray(LATTICE_WEIGHTS, jnp.float32).reshape((19, 1, 1, 1))
    return weights * density[None] * (1.0 + noise)


def draw_populations(key, part):
    return lattice_field(jax.random.fold_in(key, 11), (Q, NX, NY, NZ))


def draw_coarse_pops(key, part):
    return lattice_field(jax.random.fold_in(key, 12), (Q, NX // 2, NY // 2, NZ // 2))


def draw_bead_data(key, part):
    owners = N_GX * N_GY
    shape = (N_GX, N_GY, N_GZ, 1, owners * SLOT)
    keys = jax.random.split(jax.random.fold_in(key, 13), 5)
    first = jax.random.uniform(keys[0], shape, jnp.float32, -0.5, 1.5)
    second = jax.random.uniform(keys[1], shape, jnp.float32, -0.5, 1.5)
    third = jax.random.uniform(keys[2], shape, jnp.float32, -0.5, BIN_Z - 0.5)
    forces = 0.02 * jnp.clip(jax.random.normal(keys[3], (N_GX, N_GY, N_GZ, 3, owners * SLOT), jnp.float32), -4.0, 4.0)
    return jnp.concatenate([first, second, third, forces], axis=3)


def draw_bead_bins(key, part):
    owners = N_GX * N_GY
    bins_count = NX // N_GX // 2 * (NY // N_GY // 2) * (NZ // N_GZ // BIN_Z)
    keys = jax.random.split(jax.random.fold_in(key, 14), 5)
    load = jax.random.randint(keys[0], (owners,), 1, 5)
    counts = jax.random.randint(keys[1], (N_GX, N_GY, N_GZ, owners), 0, SLOT + 1)
    counts = jnp.minimum(SLOT, counts * load // 2)
    full_owner = jax.random.randint(keys[2], (), 0, owners)
    counts = jnp.where(jnp.arange(owners) == full_owner, SLOT, counts)
    first = jax.random.randint(keys[3], (N_GX, N_GY, N_GZ, owners, SLOT), 0, bins_count)
    second = jax.random.randint(keys[4], (N_GX, N_GY, N_GZ, owners, SLOT), 0, bins_count)
    chosen = jnp.minimum(first, second)
    live = jnp.arange(SLOT)[None, None, None, None, :] < counts[..., None]
    result = jnp.where(live, chosen, -1).astype(jnp.int32)
    return result.reshape(N_GX, N_GY, N_GZ, 1, owners * SLOT)


def place_ends(values, key, least, high):
    longest = values.shape.index(max(values.shape))
    spots = []
    for shift in (0, 1):
        where = [jax.random.randint(jax.random.fold_in(key, axis), (), 0, length) for axis, length in enumerate(values.shape)]
        where[longest] = (where[longest] + shift) % values.shape[longest]
        spots.append(tuple(where))
    return values.at[spots[0]].set(least).at[spots[1]].set(high)


def setup_inputs(seed: int = 0) -> dict:
    splits = jax.random.split(jax.random.key(seed), 7)
    populations = draw_populations(jax.random.fold_in(splits[6], 71), 0)
    coarse_pops = draw_coarse_pops(jax.random.fold_in(splits[6], 71), 0)
    fine_mask = place_ends((jax.random.randint(splits[2], (NX, NY, NZ), 0, 4) < 3).astype(jnp.int32), jax.random.fold_in(splits[2], 1), 0, 1)
    coarse_mask = place_ends((jax.random.randint(splits[3], (NX // 2, NY // 2, NZ // 2), 0, 2) < 1).astype(jnp.int32), jax.random.fold_in(splits[3], 1), 0, 1)
    bead_data = draw_bead_data(jax.random.fold_in(splits[6], 71), 0)
    bead_bins = draw_bead_bins(jax.random.fold_in(splits[6], 71), 0)
    return {"populations": populations, "coarse_pops": coarse_pops, "fine_mask": fine_mask, "coarse_mask": coarse_mask, "bead_data": bead_data, "bead_bins": bead_bins}


VELOCITIES = np.array([[0, 0, 0], [1, 0, 0], [-1, 0, 0], [0, 1, 0], [0, -1, 0], [0, 0, 1], [0, 0, -1], [1, 1, 0], [-1, -1, 0], [1, -1, 0], [-1, 1, 0], [1, 0, 1], [-1, 0, -1], [1, 0, -1], [-1, 0, 1], [0, 1, 1], [0, -1, -1], [0, 1, -1], [0, -1, 1]])
LATTICE_WEIGHTS = np.array([1.0 / 3.0] + [1.0 / 18.0] * 6 + [1.0 / 36.0] * 12)
TAU_FINE = 1.2
TAU_COARSE = 0.85
TO_COARSE = 2.0 * TAU_COARSE / TAU_FINE
TO_FINE = TAU_FINE / (2.0 * TAU_COARSE)


def weights_like(field):
    return jnp.asarray(LATTICE_WEIGHTS, field.dtype).reshape((19,) + (1,) * (field.ndim - 1))


def moments(pops):
    table = jnp.asarray(VELOCITIES, pops.dtype)
    density = jnp.sum(pops, axis=0)
    momentum = jnp.tensordot(table.T, pops, axes=1, precision=lax.Precision.HIGHEST)
    return density, momentum


def equilibrium(density, velocity, like):
    table = jnp.asarray(VELOCITIES, like.dtype)
    along = jnp.tensordot(table, velocity, axes=1, precision=lax.Precision.HIGHEST)
    speed = jnp.sum(velocity * velocity, axis=0)
    return weights_like(like) * density * (1.0 + 3.0 * along + 4.5 * along * along - 1.5 * speed)


def rescale(pops, factor):
    density, momentum = moments(pops)
    balance = equilibrium(density, momentum / density, pops)
    return balance + factor * (pops - balance)


def collide(pops, force, tau):
    density, momentum = moments(pops)
    if force is None:
        velocity = momentum / density
        return pops - (pops - equilibrium(density, velocity, pops)) / tau
    table = jnp.asarray(VELOCITIES, pops.dtype)
    velocity = (momentum + 0.5 * force) / density
    balance = equilibrium(density, velocity, pops)
    along = jnp.tensordot(table, velocity, axes=1, precision=lax.Precision.HIGHEST)
    pushed = jnp.tensordot(table, force, axes=1, precision=lax.Precision.HIGHEST)
    work = jnp.sum(velocity * force, axis=0)
    source = (1.0 - 0.5 / tau) * weights_like(pops) * (3.0 * (pushed - work) + 9.0 * along * pushed)
    return pops - (pops - balance) / tau + source


def kernel_window(start, position, cells, span, live, dtype):
    index = jnp.arange(cells).astype(jnp.int32)[None, :]
    offset = index - start[:, None]
    inside = (offset >= 0) & (offset < span) & live[:, None]
    distance = offset.astype(dtype) - position[:, None]
    return jnp.where(inside, jnp.exp(-0.5 * distance * distance), jnp.zeros_like(distance))


def spread_beads(data, bins, cells_x, cells_y, cells_z):
    nby, nbz = cells_y // 2, cells_z // BIN_Z
    count = data.shape[1]
    live = bins >= 0
    safe = jnp.maximum(bins, 0).astype(jnp.int32)
    block_x = safe // (nby * nbz)
    block_y = (safe // nbz) % nby
    block_z = safe % nbz
    kernel_x = kernel_window(2 * block_x, data[0], cells_x, 2, live, data.dtype)
    kernel_y = kernel_window(2 * block_y, data[1], cells_y, 2, live, data.dtype)
    kernel_z = kernel_window(BIN_Z * block_z, data[2], cells_z, BIN_Z, live, data.dtype)
    plane = (kernel_x[:, :, None] * kernel_y[:, None, :]).reshape(count, cells_x * cells_y)
    loaded = (data[3:6].T[:, :, None] * plane[:, None, :]).reshape(count, 3 * cells_x * cells_y)
    summed = lax.dot_general(loaded, kernel_z, (((0,), (0,)), ((), ())), precision=lax.Precision.HIGHEST)
    return summed.reshape(3, cells_x, cells_y, cells_z)


def expand_parent(parent):
    q, a, b, c = parent.shape
    grown = jnp.broadcast_to(parent[:, :, None, :, None, :, None], (q, a, 2, b, 2, c, 2))
    return grown.reshape(q, 2 * a, 2 * b, 2 * c)


def stream_periodic(post):
    moved = [jnp.roll(post[i], tuple(int(v) for v in VELOCITIES[i]), axis=(0, 1, 2)) for i in range(19)]
    return jnp.stack(moved)


def reference(populations, coarse_pops, fine_mask, coarse_mask, bead_data, bead_bins):
    owners = N_GX * N_GY
    cells_x, cells_y, cells_z = NX // N_GX, NY // N_GY, NZ // N_GZ
    data = bead_data.reshape(owners, N_GZ, 6, owners, SLOT).transpose(3, 1, 2, 0, 4).reshape(owners * N_GZ, 6, owners * SLOT)
    bins = bead_bins.reshape(owners, N_GZ, owners, SLOT).transpose(2, 1, 0, 3).reshape(owners * N_GZ, owners * SLOT)
    pieces = lax.map(lambda item: spread_beads(item[0], item[1], cells_x, cells_y, cells_z), (data, bins))
    pieces = pieces.reshape(N_GX, N_GY, N_GZ, 3, cells_x, cells_y, cells_z).transpose(3, 0, 4, 1, 5, 2, 6)
    force = pieces.reshape(3, NX, NY, NZ)
    restricted = populations.reshape(19, NX // 2, 2, NY // 2, 2, NZ // 2, 2).mean(axis=(2, 4, 6))
    coarse_pre = jnp.where(coarse_mask[None] == 1, rescale(restricted, TO_COARSE), coarse_pops)
    parent = expand_parent(rescale(coarse_pre, TO_FINE))
    fine_pre = jnp.where(fine_mask[None] == 1, populations, parent)
    fine_post = collide(fine_pre, force, TAU_FINE)
    fine_out = stream_periodic(fine_post)
    coarse_post = collide(coarse_pre, None, TAU_COARSE)
    coarse_out = stream_periodic(coarse_post)
    return fine_out, coarse_out
```

```python
import functools

import jax
import jax.numpy as jnp
import numpy as np
from jax import lax
from jax.experimental import pallas as pl
from jax.experimental.pallas import tpu as pltpu
from jax.sharding import PartitionSpec as P

BIN_Z = 32
VELOCITIES = [
    (0, 0, 0), (1, 0, 0), (-1, 0, 0), (0, 1, 0), (0, -1, 0), (0, 0, 1), (0, 0, -1),
    (1, 1, 0), (-1, -1, 0), (1, -1, 0), (-1, 1, 0), (1, 0, 1), (-1, 0, -1), (1, 0, -1),
    (-1, 0, 1), (0, 1, 1), (0, -1, -1), (0, 1, -1), (0, -1, 1),
]
WEIGHTS = [1.0 / 3.0] + [1.0 / 18.0] * 6 + [1.0 / 36.0] * 12
TAU_FINE = 1.2
TAU_COARSE = 0.85
TO_COARSE = 2.0 * TAU_COARSE / TAU_FINE
TO_FINE = TAU_FINE / (2.0 * TAU_COARSE)
LANES = 128
MESH = pl.DeviceIdType.MESH
SIGNS = (1, -1)
FACE = {(a, s): [i for i in range(19) if VELOCITIES[i][a] == s] for a in range(3) for s in SIGNS}
FACES = [(a, s) for a in range(3) for s in SIGNS]
EDGES = [i for i in range(7, 19)]


def along(vector, c):
    total = None
    for part, sign in zip(vector, c):
        if sign:
            total = part if total is None else (total + part if sign > 0 else total - part)
    return total


def moments(p):
    rho = p[0]
    sums = [None] * 19
    m = [None] * 3
    for i in range(1, 19, 2):
        rho = rho + (p[i] + p[i + 1])
        sums[i] = p[i] - p[i + 1]
        for axis, sign in enumerate(VELOCITIES[i]):
            if sign:
                if m[axis] is None:
                    m[axis] = sums[i]
                else:
                    m[axis] = m[axis] + sums[i] if sign > 0 else m[axis] - sums[i]
    return rho, m


def relax(p, rho, u, a, b, force=None, k=0.0):
    scaled = b * rho
    base = scaled * (1.0 - 1.5 * (u[0] * u[0] + u[1] * u[1] + u[2] * u[2]))
    lin = [3.0 * scaled * v for v in u]
    quad = [4.5 * scaled * v for v in u]
    if force is not None:
        base = base - (3.0 * k) * (u[0] * force[0] + u[1] * force[1] + u[2] * force[2])
        lin = [v + (3.0 * k) * f for v, f in zip(lin, force)]
        quad = [v + (9.0 * k) * f for v, f in zip(quad, force)]
    out = [None] * 19
    out[0] = a * p[0] + WEIGHTS[0] * base
    for i in range(1, 19, 2):
        c, w = VELOCITIES[i], WEIGHTS[i]
        even = w * (base + along(u, c) * along(quad, c))
        odd = w * along(lin, c)
        out[i] = a * p[i] + (even + odd)
        out[i + 1] = a * p[i + 1] + (even - odd)
    return out


def parts(x):
    high = x.astype(jnp.bfloat16)
    return high, (x - high.astype(jnp.float32)).astype(jnp.bfloat16)


def times_exact(x, table):
    high, low = parts(x)
    dot = functools.partial(jnp.dot, preferred_element_type=jnp.float32)
    return dot(high, table) + dot(low, table)


def moved(plane, c):
    rows, lanes = plane.shape
    if c[1]:
        plane = pltpu.roll(plane, 1 if c[1] > 0 else rows - 1, 0)
    if c[2]:
        plane = pltpu.roll(plane, 1 if c[2] > 0 else lanes - 1, 1)
    return plane


def kernel(
    sizes, slots, pop_in, cpop_in, fmask_in, cmask_in, bead_ref, bins_ref, fine_out, coarse_out,
    pops, cpops, fmask, cmask, summed, restricted, parent, wide, tall, force, stream, cstream,
    bead_send, bead_recv, bead_tiles, xs, ys, zs, xr, yr, zr, er_y, er_z,
    in_sem, out_sem, bead_sem, send_sem, recv_sem,
):
    ngx, ngy, ngz = sizes
    gx, gy, gz = lax.axis_index("gx"), lax.axis_index("gy"), lax.axis_index("gz")
    owners = ngx * ngy
    me = gx * ngy + gy
    _, nx, ny, nz = pops.shape
    _, hx, hy, hz = cpops.shape
    chunks = bins_ref.shape[0]
    per = LANES // slots

    loads = [
        pltpu.make_async_copy(src, dst, in_sem.at[n])
        for n, (src, dst) in enumerate(
            ((pop_in, pops), (cpop_in, cpops), (fmask_in, fmask), (cmask_in, cmask))
        )
    ]
    for load in loads:
        load.start()

    def device(offset):
        return (
            lax.rem(gx + (offset[0] + ngx), ngx),
            lax.rem(gy + (offset[1] + ngy), ngy),
            lax.rem(gz + (offset[2] + ngz), ngz),
        )

    def owner(step):
        other = lax.rem(me + step, owners)
        return other, (other // ngy, lax.rem(other, ngy), gz)

    barrier = pltpu.get_barrier_semaphore()
    cross = [(0, 0, 1), (0, 0, -1)] + [VELOCITIES[i] for i in EDGES if VELOCITIES[i][2]]
    for offset in cross:
        pl.semaphore_signal(barrier, inc=1, device_id=device(offset), device_id_type=MESH)

    @pl.loop(1, owners)
    def _(step):
        pl.semaphore_signal(barrier, inc=1, device_id=owner(step)[1], device_id_type=MESH)

    for chunk in range(chunks):
        bead_send[chunk, 0:6, :] = bead_ref[pl.ds(chunk, 6, stride=chunks), :]
        bead_send[chunk, 6:7, :] = bins_ref[chunk : chunk + 1, :].astype(jnp.float32)
        bead_send[chunk, 7:8, :] = jnp.zeros((1, LANES), jnp.float32)
    bead_recv[me] = bead_send[me // per]

    pl.semaphore_wait(barrier, len(cross) + owners - 1)

    @pl.loop(1, owners)
    def _(step):
        other, where = owner(step)
        pltpu.make_async_remote_copy(
            src_ref=bead_send.at[other // per],
            dst_ref=bead_recv.at[me],
            send_sem=bead_sem.at[0],
            recv_sem=bead_sem.at[1],
            device_id=where,
            device_id_type=MESH,
        ).start()

    for load in loads:
        load.wait()

    @pl.loop(0, 19)
    def _(q):
        for x in range(hx):
            total = None
            for i in range(2):
                for j in range(2):
                    piece = pops[q, 2 * x + i, pl.ds(j, hy, stride=2), :]
                    total = piece if total is None else total + piece
            summed[q, x] = total

    fold = lax.broadcasted_iota(jnp.int32, (nz, hz), 0) - 2 * lax.broadcasted_iota(
        jnp.int32, (nz, hz), 1
    )
    fold = jnp.where((fold == 0) | (fold == 1), 0.125, 0.0).astype(jnp.bfloat16)
    restricted[...] = times_exact(summed[...].reshape(19 * hx * hy, nz), fold).reshape(
        19, hx, hy, hz
    )

    @pl.loop(0, hx)
    def _(x):
        p = [restricted[i, x] for i in range(19)]
        rho, m = moments(p)
        inv = 1.0 / rho
        pre = relax(p, rho, [v * inv for v in m], TO_COARSE, 1.0 - TO_COARSE)
        live = cmask[x] == 1
        pre = [jnp.where(live, pre[i], cpops[i, x]) for i in range(19)]
        rho, m = moments(pre)
        inv = 1.0 / rho
        u = [v * inv for v in m]
        down = relax(pre, rho, u, TO_FINE, 1.0 - TO_FINE)
        post = relax(pre, rho, u, 1.0 - 1.0 / TAU_COARSE, 1.0 / TAU_COARSE)
        for i in range(19):
            c = VELOCITIES[i]
            parent[i, x] = down[i]
            cstream[i, lax.rem(x + (c[0] + hx), hx)] = moved(post[i], c)

    spread = lax.broadcasted_iota(jnp.int32, (hz, nz), 1) - 2 * lax.broadcasted_iota(
        jnp.int32, (hz, nz), 0
    )
    spread = jnp.where((spread == 0) | (spread == 1), 1.0, 0.0).astype(jnp.bfloat16)
    wide[...] = times_exact(parent[...].reshape(19 * hx * hy, hz), spread).reshape(19, hx, hy, nz)

    @pl.loop(0, 19)
    def _(q):
        for x in range(hx):
            value = wide[q, x]
            tall[x, pl.ds(0, hy, stride=2), :] = value
            tall[x, pl.ds(1, hy, stride=2), :] = value
        for x in range(nx):
            pops[q, x] = jnp.where(fmask[x] == 1, pops[q, x], tall[x // 2])

    lane_c = lax.broadcasted_iota(jnp.int32, (hy, LANES), 1)
    for a, s in FACES:
        slot = 0 if s > 0 else 1
        if a == 2:
            packed = jnp.zeros((hy, LANES), jnp.float32)
        for j, i in enumerate(FACE[a, s]):
            if a == 0:
                xs[slot, j, ny:, 0:hz] = cstream[i, 0 if s > 0 else hx - 1]
            elif a == 1:
                row = 0 if s > 0 else hy - 1
                for x in range(hx):
                    ys[slot, j, nx + x : nx + x + 1, 0:hz] = cstream[i, x, row : row + 1, :]
            else:
                col = 0 if s > 0 else hz - 1
                for x in range(hx):
                    packed = jnp.where(
                        lane_c == j * hx + x, cstream[i, x, :, col : col + 1], packed
                    )
        if a == 2:
            zs[slot, ny:, :] = packed

    arrived = bead_recv.at[pl.ds(0, owners - 1)]
    pltpu.make_async_copy(arrived, arrived, bead_sem.at[1]).wait()
    lane = lax.broadcasted_iota(jnp.int32, (8, LANES), 1)
    mine = lax.rem(me, per)

    @pl.loop(0, owners // per)
    def _(t):
        tile = jnp.zeros((8, LANES), jnp.float32)
        for k in range(per):
            turned = pltpu.roll(
                bead_recv[t * per + k], lax.rem((k + per - mine) * slots, LANES), 1
            )
            tile = jnp.where((lane >= k * slots) & (lane < (k + 1) * slots), turned, tile)
        bead_tiles[t] = tile

    force[...] = jnp.zeros_like(force)
    bins_y, bins_z = ny // 2, nz // BIN_Z

    def window(start, position, live, cells, span):
        offset = lax.broadcasted_iota(jnp.int32, (cells, LANES), 0).astype(jnp.float32) - start
        distance = offset - position
        inside = (offset >= 0.0) & (offset < span) & live
        return jnp.where(inside, jnp.exp(-0.5 * distance * distance), 0.0)

    @pl.loop(0, owners // per)
    def _(t):
        tile = bead_tiles[t]
        number = tile[6:7]
        live = number >= 0.0
        bx = jnp.floor((number + 0.5) * (1.0 / (bins_y * bins_z)))
        rest = number - bx * (bins_y * bins_z)
        by = jnp.floor((rest + 0.5) * (1.0 / bins_z))
        bz = rest - by * bins_z
        wx = window(2.0 * bx, tile[0:1], live, nx, 2.0)
        wy = window(2.0 * by, tile[1:2], live, ny, 2.0)
        wz = window(float(BIN_Z) * bz, tile[2:3], live, nz, float(BIN_Z))
        rows = []
        for d in range(3):
            pushed = wx * tile[3 + d : 4 + d]
            for x in range(nx):
                rows.append(pushed[x : x + 1] * wy)
        left = jnp.concatenate(rows, axis=0)
        lh, ll = parts(left)
        rh, rl = parts(wz)
        total = lax.dot_general(
            jnp.concatenate([lh, lh, ll], axis=1),
            jnp.concatenate([rh, rl, rh], axis=1),
            (((1,), (1,)), ((), ())),
            preferred_element_type=jnp.float32,
        )
        force[...] += total.reshape(3, nx, ny, nz)

    @pl.loop(0, nx)
    def _(x):
        p = [pops[i, x] for i in range(19)]
        f = [force[d, x] for d in range(3)]
        rho, m = moments(p)
        inv = 1.0 / rho
        u = [(v + 0.5 * w) * inv for v, w in zip(m, f)]
        post = relax(
            p, rho, u, 1.0 - 1.0 / TAU_FINE, 1.0 / TAU_FINE, f, 1.0 - 0.5 / TAU_FINE
        )
        for i in range(19):
            c = VELOCITIES[i]
            stream[i, lax.rem(x + (c[0] + nx), nx)] = moved(post[i], c)

    lane_f = lax.broadcasted_iota(jnp.int32, (ny, LANES), 1)
    for a, s in FACES:
        slot = 0 if s > 0 else 1
        for j, i in enumerate(FACE[a, s]):
            if a == 0:
                xs[slot, j, 0:ny, :] = stream[i, 0 if s > 0 else nx - 1]
            elif a == 1:
                row = 0 if s > 0 else ny - 1
                for x in range(nx):
                    ys[slot, j, x : x + 1, :] = stream[i, x, row : row + 1, :]
        if a == 2:
            col = 0 if s > 0 else nz - 1

            def pack(x, packed):
                for j, i in enumerate(FACE[a, s]):
                    packed = jnp.where(
                        lane_f == j * nx + x, stream[i, x, :, col : col + 1], packed
                    )
                return packed

            zs[slot, 0:ny, :] = lax.fori_loop(0, nx, pack, jnp.zeros((ny, LANES), jnp.float32))

    copies = []

    def send(src, dst, offset):
        n = len(copies)
        copy = pltpu.make_async_remote_copy(
            src_ref=src, dst_ref=dst, send_sem=send_sem.at[n], recv_sem=recv_sem.at[n],
            device_id=device(offset), device_id_type=MESH,
        )
        copy.start()
        copies.append(copy)

    for a, s in FACES:
        slot = 0 if s > 0 else 1
        offset = tuple(s if axis == a else 0 for axis in range(3))
        src, dst = ((xs, xr), (ys, yr), (zs, zr))[a]
        send(src.at[slot], dst.at[slot], offset)
    for n, i in enumerate(EDGES):
        c = VELOCITIES[i]
        if c[2]:
            send(zs.at[0 if c[2] > 0 else 1], er_z.at[n - 4], c)
        else:
            slot = 0 if c[1] > 0 else 1
            send(ys.at[slot, FACE[1, c[1]].index(i)], er_y.at[n], c)
    pltpu.make_async_copy(arrived, arrived, bead_sem.at[0]).wait()
    for copy in copies:
        copy.wait()

    def side(sign, length):
        return 0 if sign > 0 else length - 1

    for target, rows_y, shape in (
        (stream, slice(0, ny), (nx, ny, nz)),
        (cstream, slice(ny, ny + hy), (hx, hy, hz)),
    ):
        fx, fy, fz = shape
        first = 0 if target is stream else nx
        low = 0 if target is stream else ny
        lane_t = lax.broadcasted_iota(jnp.int32, (fy, LANES), 1)
        row_t = lax.broadcasted_iota(jnp.int32, (fy, LANES), 0)
        for s in SIGNS:
            for j, i in enumerate(FACE[0, s]):
                target[i, side(s, fx)] = xr[0 if s > 0 else 1, j, rows_y, 0:fz]
        for s in SIGNS:
            for j, i in enumerate(FACE[1, s]):
                c = VELOCITIES[i]
                y = side(s, fy)
                for x in range(fx):
                    src = yr.at[0 if s > 0 else 1, j]
                    if c[0] and x == side(c[0], fx):
                        src = er_y.at[EDGES.index(i)]
                    target[i, x, y : y + 1, :] = src[first + x : first + x + 1, 0:fz]
        for s in SIGNS:
            column = zr[0 if s > 0 else 1, low : low + fy, :]
            for j, i in enumerate(FACE[2, s]):
                c = VELOCITIES[i]
                if c[0]:
                    spot = lane_t == j * fx + side(c[0], fx)
                elif c[1]:
                    spot = (
                        (lane_t >= j * fx) & (lane_t < (j + 1) * fx) & (row_t == side(c[1], fy))
                    )
                else:
                    continue
                column = jnp.where(spot, er_z[EDGES.index(i) - 4, low : low + fy, :], column)
            edge = lax.broadcasted_iota(jnp.int32, (fy, fz), 1) == side(s, fz)
            for j, i in enumerate(FACE[2, s]):
                for x in range(fx):
                    k = j * fx + x
                    target[i, x] = jnp.where(edge, column[:, k : k + 1], target[i, x])

    stores = [
        pltpu.make_async_copy(stream, fine_out, out_sem.at[0]),
        pltpu.make_async_copy(cstream, coarse_out, out_sem.at[1]),
    ]
    for store in stores:
        store.start()
    for store in stores:
        store.wait()


def local(populations, coarse_pops, fine_mask, coarse_mask, bead_data, bead_bins):
    _, nx, ny, nz = populations.shape
    _, hx, hy, hz = coarse_pops.shape
    sizes = tuple(lax.axis_size(axis) for axis in ("gx", "gy", "gz"))
    owners = sizes[0] * sizes[1]
    total = bead_data.shape[4]
    chunks = total // LANES
    slots = total // owners
    beads = bead_data.reshape(6 * chunks, LANES)
    bins = bead_bins.reshape(chunks, LANES)
    f32, i32 = jnp.float32, jnp.int32
    rows = nx + 8 * ((hx + 7) // 8)
    any_spec = pl.BlockSpec(memory_space=pl.ANY)
    vmem_spec = pl.BlockSpec(memory_space=pltpu.VMEM)
    dma = pltpu.SemaphoreType.DMA
    return pl.pallas_call(
        functools.partial(kernel, sizes, slots),
        out_shape=(
            jax.ShapeDtypeStruct(populations.shape, f32),
            jax.ShapeDtypeStruct(coarse_pops.shape, f32),
        ),
        in_specs=[any_spec] * 4 + [vmem_spec] * 2,
        out_specs=(any_spec, any_spec),
        scratch_shapes=[
            pltpu.VMEM((19, nx, ny, nz), f32),
            pltpu.VMEM((19, hx, hy, hz), f32),
            pltpu.VMEM((nx, ny, nz), i32),
            pltpu.VMEM((hx, hy, hz), i32),
            pltpu.VMEM((19, hx, hy, nz), f32),
            pltpu.VMEM((19, hx, hy, hz), f32),
            pltpu.VMEM((19, hx, hy, hz), f32),
            pltpu.VMEM((19, hx, hy, nz), f32),
            pltpu.VMEM((hx, ny, nz), f32),
            pltpu.VMEM((3, nx, ny, nz), f32),
            pltpu.VMEM((19, nx, ny, nz), f32),
            pltpu.VMEM((19, hx, hy, hz), f32),
            pltpu.VMEM((chunks, 8, LANES), f32),
            pltpu.VMEM((owners, 8, LANES), f32),
            pltpu.VMEM((total // LANES, 8, LANES), f32),
            pltpu.VMEM((2, 5, ny + hy, LANES), f32),
            pltpu.VMEM((2, 5, rows, LANES), f32),
            pltpu.VMEM((2, ny + hy, LANES), f32),
            pltpu.VMEM((2, 5, ny + hy, LANES), f32),
            pltpu.VMEM((2, 5, rows, LANES), f32),
            pltpu.VMEM((2, ny + hy, LANES), f32),
            pltpu.VMEM((4, rows, LANES), f32),
            pltpu.VMEM((8, ny + hy, LANES), f32),
            dma((4,)),
            dma((2,)),
            dma((2,)),
            dma((18,)),
            dma((18,)),
        ],
        compiler_params=pltpu.CompilerParams(collective_id=0, has_side_effects=True),
    )(populations, coarse_pops, fine_mask, coarse_mask, beads, bins)


def solution(mesh):
    in_specs = (
        P(None, "gx", "gy", "gz"),
        P(None, "gx", "gy", "gz"),
        P("gx", "gy", "gz"),
        P("gx", "gy", "gz"),
        P("gx", "gy", "gz", None, None),
        P("gx", "gy", "gz", None, None),
    )
    out_specs = (P(None, "gx", "gy", "gz"), P(None, "gx", "gy", "gz"))
    return jax.shard_map(local, mesh=mesh, in_specs=in_specs, out_specs=out_specs, check_vma=False)
```

```python
import functools

import jax
import jax.numpy as jnp
import numpy as np
from jax import lax
from jax.experimental import pallas as pl
from jax.experimental.pallas import tpu as pltpu
from jax.sharding import PartitionSpec as P

BIN_Z = 32
VELOCITIES = [
    (0, 0, 0), (1, 0, 0), (-1, 0, 0), (0, 1, 0), (0, -1, 0), (0, 0, 1), (0, 0, -1),
    (1, 1, 0), (-1, -1, 0), (1, -1, 0), (-1, 1, 0), (1, 0, 1), (-1, 0, -1), (1, 0, -1),
    (-1, 0, 1), (0, 1, 1), (0, -1, -1), (0, 1, -1), (0, -1, 1),
]
WEIGHTS = [1.0 / 3.0] + [1.0 / 18.0] * 6 + [1.0 / 36.0] * 12
TAU_FINE = 1.2
TAU_COARSE = 0.85
TO_COARSE = 2.0 * TAU_COARSE / TAU_FINE
TO_FINE = TAU_FINE / (2.0 * TAU_COARSE)
LANES = 128
LIMIT = 24 * 2**20
MESH = pl.DeviceIdType.MESH
SIGNS = (1, -1)
FACE = {(a, s): [i for i in range(19) if VELOCITIES[i][a] == s] for a in range(3) for s in SIGNS}
FACES = [(a, s) for a in range(3) for s in SIGNS]
EDGES = [i for i in range(7, 19)]


def along(vector, c):
    total = None
    for part, sign in zip(vector, c):
        if sign:
            total = part if total is None else (total + part if sign > 0 else total - part)
    return total


def moments(p):
    rho = p[0]
    sums = [None] * 19
    m = [None] * 3
    for i in range(1, 19, 2):
        rho = rho + (p[i] + p[i + 1])
        sums[i] = p[i] - p[i + 1]
        for axis, sign in enumerate(VELOCITIES[i]):
            if sign:
                if m[axis] is None:
                    m[axis] = sums[i]
                else:
                    m[axis] = m[axis] + sums[i] if sign > 0 else m[axis] - sums[i]
    return rho, m


def relax(p, rho, u, a, b, force=None, k=0.0):
    scaled = b * rho
    base = scaled * (1.0 - 1.5 * (u[0] * u[0] + u[1] * u[1] + u[2] * u[2]))
    lin = [3.0 * scaled * v for v in u]
    quad = [4.5 * scaled * v for v in u]
    if force is not None:
        base = base - (3.0 * k) * (u[0] * force[0] + u[1] * force[1] + u[2] * force[2])
        lin = [v + (3.0 * k) * f for v, f in zip(lin, force)]
        quad = [v + (9.0 * k) * f for v, f in zip(quad, force)]
    out = [None] * 19
    out[0] = a * p[0] + WEIGHTS[0] * base
    for i in range(1, 19, 2):
        c, w = VELOCITIES[i], WEIGHTS[i]
        even = w * (base + along(u, c) * along(quad, c))
        odd = w * along(lin, c)
        out[i] = a * p[i] + (even + odd)
        out[i + 1] = a * p[i + 1] + (even - odd)
    return out


def parts(x):
    high = x.astype(jnp.bfloat16)
    return high, (x - high.astype(jnp.float32)).astype(jnp.bfloat16)


def times_exact(x, table):
    high, low = parts(x)
    dot = functools.partial(jnp.dot, preferred_element_type=jnp.float32)
    return dot(high, table) + dot(low, table)


def moved(plane, c):
    rows, lanes = plane.shape
    if c[1]:
        plane = pltpu.roll(plane, 1 if c[1] > 0 else rows - 1, 0)
    if c[2]:
        plane = pltpu.roll(plane, 1 if c[2] > 0 else lanes - 1, 1)
    return plane


def side(sign, length):
    return 0 if sign > 0 else length - 1


def slot_of(sign):
    return 0 if sign > 0 else 1


def pack_x(target, xs, es):
    _, fx, fy, fz = target.shape
    row = lax.broadcasted_iota(jnp.int32, (fy, LANES), 0)
    diagonal = row == lax.broadcasted_iota(jnp.int32, (fy, LANES), 1)
    for s in SIGNS:
        for j, i in enumerate(FACE[0, s]):
            plane = target[i, side(s, fx)]
            xs[slot_of(s), j] = plane
            c = VELOCITIES[i]
            if c[1]:
                y = side(c[1], fy)
                es[EDGES.index(i), :, 0:fz] = plane[y : y + 1]
            elif c[2]:
                z = side(c[2], fz)
                turned = jnp.where(diagonal, plane[:, z : z + 1], 0.0)
                es[EDGES.index(i)] = jnp.sum(turned, axis=0, keepdims=True)


def pack_yz(target, ys, zs, es):
    _, fx, fy, fz = target.shape
    lane = lax.broadcasted_iota(jnp.int32, (fy, LANES), 1)
    for s in SIGNS:
        y, z = side(s, fy), side(s, fz)
        for j, i in enumerate(FACE[1, s]):
            for x in range(fx):
                ys[slot_of(s), j * fx + x : j * fx + x + 1, :] = target[i, x, y : y + 1, :]
        packed = jnp.zeros((fy, LANES), jnp.float32)
        for j, i in enumerate(FACE[2, s]):
            for x in range(fx):
                packed = jnp.where(lane == j * fx + x, target[i, x, :, z : z + 1], packed)
        zs[slot_of(s)] = packed
        for i in FACE[2, s]:
            c = VELOCITIES[i]
            if c[1]:
                y = side(c[1], fy)
                es[EDGES.index(i)] = packed[y : y + 1]


def finish(*refs):
    levels = (refs[0:5], refs[5:10])
    outs, targets, store_sem = refs[10:12], refs[12:14], refs[14]
    stores = []
    for n in (0, 1):
        target = targets[n]
        source, xr, yr, zr, er = levels[n]
        _, fx, fy, fz = target.shape
        lane = lax.broadcasted_iota(jnp.int32, (fy, LANES), 1)
        row = lax.broadcasted_iota(jnp.int32, (fy, LANES), 0)
        last = lax.broadcasted_iota(jnp.int32, (fy, fz), 1)
        columns = []
        for s in SIGNS:
            column = zr[slot_of(s)]
            for j, i in enumerate(FACE[2, s]):
                c = VELOCITIES[i]
                if c[0]:
                    value = jnp.sum(
                        jnp.where(row == lane, er[EDGES.index(i)], 0.0), axis=1, keepdims=True
                    )
                    column = jnp.where(lane == j * fx + side(c[0], fx), value, column)
                elif c[1]:
                    spot = (lane >= j * fx) & (lane < (j + 1) * fx) & (row == side(c[1], fy))
                    column = jnp.where(spot, er[EDGES.index(i)], column)
            columns.append(column)
        for i in range(19):
            c = VELOCITIES[i]
            target[i] = source[i]
            if c[0]:
                target[i, side(c[0], fx)] = xr[slot_of(c[0]), FACE[0, c[0]].index(i)]
            if c[1]:
                y, j = side(c[1], fy), FACE[1, c[1]].index(i)
                for x in range(fx):
                    if c[0] and x == side(c[0], fx):
                        piece = er[EDGES.index(i), :, 0:fz]
                    else:
                        piece = yr[slot_of(c[1]), j * fx + x : j * fx + x + 1, :]
                    target[i, x, y : y + 1, :] = piece
            if c[2]:
                j, column = FACE[2, c[2]].index(i), columns[slot_of(c[2])]
                for x in range(fx):
                    k = j * fx + x
                    target[i, x] = jnp.where(
                        last == side(c[2], fz), column[:, k : k + 1], target[i, x]
                    )
            store = pltpu.make_async_copy(target.at[i], outs[n].at[i], store_sem.at[n, i])
            store.start()
            stores.append(store)
    for store in stores:
        store.wait()


def kernel(
    sizes, slots, pop_in, cpop_in, fmask_in, cmask_in, bead_ref, bins_ref,
    stream, fxr, fyr, fzr, fer, cstream, cxr, cyr, czr, cer,
    pops, cpops, fmask, cmask, summed, restricted, parent, wide, tall, force,
    bead_send, bead_recv, bead_tiles, fxs, fys, fzs, fes, cxs, cys, czs, ces,
    in_sem, bead_sem, send_sem, recv_sem,
):
    ngx, ngy, ngz = sizes
    gx, gy, gz = lax.axis_index("gx"), lax.axis_index("gy"), lax.axis_index("gz")
    owners = ngx * ngy
    me = gx * ngy + gy
    _, nx, ny, nz = pops.shape
    _, hx, hy, hz = cpops.shape
    chunks = bins_ref.shape[0]
    per = LANES // slots

    loads = [
        pltpu.make_async_copy(src, dst, in_sem.at[n])
        for n, (src, dst) in enumerate(
            ((pop_in, pops), (cpop_in, cpops), (fmask_in, fmask), (cmask_in, cmask))
        )
    ]
    for load in loads:
        load.start()

    def device(offset):
        return (
            lax.rem(gx + (offset[0] + ngx), ngx),
            lax.rem(gy + (offset[1] + ngy), ngy),
            lax.rem(gz + (offset[2] + ngz), ngz),
        )

    def owner(step):
        other = lax.rem(me + step, owners)
        return other, (other // ngy, lax.rem(other, ngy), gz)

    def each_peer(act):
        if owners > 32:
            pl.loop(1, owners)(act)
        else:
            for step in sorted(range(1, owners), key=lambda n: -min(n, owners - n)):
                act(step)

    barrier = pltpu.get_barrier_semaphore()
    cross = [(0, 0, 1), (0, 0, -1)] + [VELOCITIES[i] for i in EDGES if VELOCITIES[i][2]]
    for offset in cross:
        pl.semaphore_signal(barrier, inc=1, device_id=device(offset), device_id_type=MESH)

    @each_peer
    def _(step):
        pl.semaphore_signal(barrier, inc=1, device_id=owner(step)[1], device_id_type=MESH)

    for chunk in range(chunks):
        bead_send[chunk, 0:6, :] = bead_ref[pl.ds(chunk, 6, stride=chunks), :]
        bead_send[chunk, 6:7, :] = bins_ref[chunk : chunk + 1, :].astype(jnp.float32)
        bead_send[chunk, 7:8, :] = jnp.zeros((1, LANES), jnp.float32)
    bead_recv[me] = bead_send[me // per]

    pl.semaphore_wait(barrier, len(cross) + owners - 1)

    @each_peer
    def _(step):
        other, where = owner(step)
        pltpu.make_async_remote_copy(
            src_ref=bead_send.at[other // per],
            dst_ref=bead_recv.at[me],
            send_sem=bead_sem.at[0],
            recv_sem=bead_sem.at[1],
            device_id=where,
            device_id_type=MESH,
        ).start()

    for load in loads:
        load.wait()

    @pl.loop(0, 19)
    def _(q):
        for x in range(hx):
            total = None
            for i in range(2):
                for j in range(2):
                    piece = pops[q, 2 * x + i, pl.ds(j, hy, stride=2), :]
                    total = piece if total is None else total + piece
            summed[q, x] = total

    fold = lax.broadcasted_iota(jnp.int32, (nz, hz), 0) - 2 * lax.broadcasted_iota(
        jnp.int32, (nz, hz), 1
    )
    fold = jnp.where((fold == 0) | (fold == 1), 0.125, 0.0).astype(jnp.bfloat16)
    restricted[...] = times_exact(summed[...].reshape(19 * hx * hy, nz), fold).reshape(
        19, hx, hy, hz
    )

    @pl.loop(0, hx)
    def _(x):
        p = [restricted[i, x] for i in range(19)]
        rho, m = moments(p)
        inv = 1.0 / rho
        pre = relax(p, rho, [v * inv for v in m], TO_COARSE, 1.0 - TO_COARSE)
        live = cmask[x] == 1
        pre = [jnp.where(live, pre[i], cpops[i, x]) for i in range(19)]
        rho, m = moments(pre)
        inv = 1.0 / rho
        u = [v * inv for v in m]
        down = relax(pre, rho, u, TO_FINE, 1.0 - TO_FINE)
        post = relax(pre, rho, u, 1.0 - 1.0 / TAU_COARSE, 1.0 / TAU_COARSE)
        for i in range(19):
            c = VELOCITIES[i]
            parent[i, x] = down[i]
            cstream[i, lax.rem(x + (c[0] + hx), hx)] = moved(post[i], c)

    spread = lax.broadcasted_iota(jnp.int32, (hz, nz), 1) - 2 * lax.broadcasted_iota(
        jnp.int32, (hz, nz), 0
    )
    spread = jnp.where((spread == 0) | (spread == 1), 1.0, 0.0).astype(jnp.bfloat16)
    wide[...] = times_exact(parent[...].reshape(19 * hx * hy, hz), spread).reshape(19, hx, hy, nz)

    @pl.loop(0, 19)
    def _(q):
        for x in range(hx):
            value = wide[q, x]
            tall[x, pl.ds(0, hy, stride=2), :] = value
            tall[x, pl.ds(1, hy, stride=2), :] = value
        for x in range(nx):
            pops[q, x] = jnp.where(fmask[x] == 1, pops[q, x], tall[x // 2])

    copies = []

    def send(src, dst, offset):
        n = len(copies)
        copy = pltpu.make_async_remote_copy(
            src_ref=src, dst_ref=dst, send_sem=send_sem.at[n], recv_sem=recv_sem.at[n],
            device_id=device(offset), device_id_type=MESH,
        )
        copy.start()
        copies.append(copy)

    def send_x(xs, xr, es, er):
        for s in SIGNS:
            send(xs.at[slot_of(s)], xr.at[slot_of(s)], (s, 0, 0))
        for n, i in enumerate(EDGES):
            if VELOCITIES[i][0]:
                send(es.at[n], er.at[n], VELOCITIES[i])

    def send_yz(ys, yr, zs, zr, es, er):
        for s in SIGNS:
            send(ys.at[slot_of(s)], yr.at[slot_of(s)], (0, s, 0))
            send(zs.at[slot_of(s)], zr.at[slot_of(s)], (0, 0, s))
        for n, i in enumerate(EDGES):
            if not VELOCITIES[i][0]:
                send(es.at[n], er.at[n], VELOCITIES[i])

    pack_x(cstream, cxs, ces)
    send_x(cxs, cxr, ces, cer)
    pack_yz(cstream, cys, czs, ces)
    send_yz(cys, cyr, czs, czr, ces, cer)

    arrived = bead_recv.at[pl.ds(0, owners - 1)]
    pltpu.make_async_copy(arrived, arrived, bead_sem.at[1]).wait()
    lane = lax.broadcasted_iota(jnp.int32, (8, LANES), 1)
    mine = lax.rem(me, per)

    @pl.loop(0, owners // per)
    def _(t):
        tile = jnp.zeros((8, LANES), jnp.float32)
        for k in range(per):
            turned = pltpu.roll(
                bead_recv[t * per + k], lax.rem((k + per - mine) * slots, LANES), 1
            )
            tile = jnp.where((lane >= k * slots) & (lane < (k + 1) * slots), turned, tile)
        bead_tiles[t] = tile

    force[...] = jnp.zeros_like(force)
    bins_y, bins_z = ny // 2, nz // BIN_Z

    def window(start, position, live, cells, span):
        offset = lax.broadcasted_iota(jnp.int32, (cells, LANES), 0).astype(jnp.float32) - start
        distance = offset - position
        inside = (offset >= 0.0) & (offset < span) & live
        return jnp.where(inside, jnp.exp(-0.5 * distance * distance), 0.0)

    @pl.loop(0, owners // per)
    def _(t):
        tile = bead_tiles[t]
        number = tile[6:7]
        live = number >= 0.0
        bx = jnp.floor((number + 0.5) * (1.0 / (bins_y * bins_z)))
        rest = number - bx * (bins_y * bins_z)
        by = jnp.floor((rest + 0.5) * (1.0 / bins_z))
        bz = rest - by * bins_z
        wx = window(2.0 * bx, tile[0:1], live, nx, 2.0)
        wy = window(2.0 * by, tile[1:2], live, ny, 2.0)
        wz = window(float(BIN_Z) * bz, tile[2:3], live, nz, float(BIN_Z))
        rows = []
        for d in range(3):
            pushed = wx * tile[3 + d : 4 + d]
            for x in range(nx):
                rows.append(pushed[x : x + 1] * wy)
        left = jnp.concatenate(rows, axis=0)
        lh, ll = parts(left)
        rh, rl = parts(wz)
        total = lax.dot_general(
            jnp.concatenate([lh, lh, ll], axis=1),
            jnp.concatenate([rh, rl, rh], axis=1),
            (((1,), (1,)), ((), ())),
            preferred_element_type=jnp.float32,
        )
        force[...] += total.reshape(3, nx, ny, nz)

    def collide(k):
        x = lax.rem(k + (nx - 1), nx)
        p = [pops[i, x] for i in range(19)]
        f = [force[d, x] for d in range(3)]
        rho, m = moments(p)
        inv = 1.0 / rho
        u = [(v + 0.5 * w) * inv for v, w in zip(m, f)]
        post = relax(
            p, rho, u, 1.0 - 1.0 / TAU_FINE, 1.0 / TAU_FINE, f, 1.0 - 0.5 / TAU_FINE
        )
        for i in range(19):
            c = VELOCITIES[i]
            stream[i, lax.rem(x + (c[0] + nx), nx)] = moved(post[i], c)

    pl.loop(0, 2)(collide)
    pack_x(stream, fxs, fes)
    send_x(fxs, fxr, fes, fer)
    pl.loop(2, nx)(collide)
    pack_yz(stream, fys, fzs, fes)
    send_yz(fys, fyr, fzs, fzr, fes, fer)
    pltpu.make_async_copy(arrived, arrived, bead_sem.at[0]).wait()
    for copy in copies:
        copy.wait()


def local(populations, coarse_pops, fine_mask, coarse_mask, bead_data, bead_bins):
    _, nx, ny, nz = populations.shape
    _, hx, hy, hz = coarse_pops.shape
    sizes = tuple(lax.axis_size(axis) for axis in ("gx", "gy", "gz"))
    owners = sizes[0] * sizes[1]
    total = bead_data.shape[4]
    chunks = total // LANES
    slots = total // owners
    beads = bead_data.reshape(6 * chunks, LANES)
    bins = bead_bins.reshape(chunks, LANES)
    f32, i32 = jnp.float32, jnp.int32
    any_spec = pl.BlockSpec(memory_space=pl.ANY)
    hbm_spec = pl.BlockSpec(memory_space=pltpu.HBM)
    vmem_spec = pl.BlockSpec(memory_space=pltpu.VMEM)
    dma = pltpu.SemaphoreType.DMA

    def rim(fx, fy, fz):
        return [(2, 5, fy, fz), (2, 5 * fx, fz), (2, fy, LANES), (12, 1, LANES)]

    fine_rim, coarse_rim = rim(nx, ny, nz), rim(hx, hy, hz)
    shapes = [populations.shape, *fine_rim, coarse_pops.shape, *coarse_rim]
    pieces = pl.pallas_call(
        functools.partial(kernel, sizes, slots),
        out_shape=[jax.ShapeDtypeStruct(shape, f32) for shape in shapes],
        in_specs=[hbm_spec] * 4 + [vmem_spec] * 2,
        out_specs=([vmem_spec] + [any_spec] * 4) * 2,
        scratch_shapes=[
            pltpu.VMEM((19, nx, ny, nz), f32),
            pltpu.VMEM((19, hx, hy, hz), f32),
            pltpu.VMEM((nx, ny, nz), i32),
            pltpu.VMEM((hx, hy, hz), i32),
            pltpu.VMEM((19, hx, hy, nz), f32),
            pltpu.VMEM((19, hx, hy, hz), f32),
            pltpu.VMEM((19, hx, hy, hz), f32),
            pltpu.VMEM((19, hx, hy, nz), f32),
            pltpu.VMEM((hx, ny, nz), f32),
            pltpu.VMEM((3, nx, ny, nz), f32),
            pltpu.VMEM((chunks, 8, LANES), f32),
            pltpu.VMEM((owners, 8, LANES), f32),
            pltpu.VMEM((total // LANES, 8, LANES), f32),
            *[pltpu.VMEM(shape, f32) for shape in fine_rim + coarse_rim],
            dma((4,)),
            dma((2,)),
            dma((36,)),
            dma((36,)),
        ],
        compiler_params=pltpu.CompilerParams(
            collective_id=0, has_side_effects=True, vmem_limit_bytes=LIMIT
        ),
    )(*[pltpu.with_memory_space_constraint(v, pltpu.HBM) for v in (populations, coarse_pops, fine_mask, coarse_mask, beads, bins)])
    return tuple(
        pl.pallas_call(
            finish,
            out_shape=[
                jax.ShapeDtypeStruct(populations.shape, f32),
                jax.ShapeDtypeStruct(coarse_pops.shape, f32),
            ],
            in_specs=[vmem_spec] * len(shapes),
            out_specs=[any_spec] * 2,
            scratch_shapes=[
                pltpu.VMEM(populations.shape, f32),
                pltpu.VMEM(coarse_pops.shape, f32),
                dma((2, 19)),
            ],
            compiler_params=pltpu.CompilerParams(vmem_limit_bytes=LIMIT),
        )(*pieces)
    )


def solution(mesh):
    in_specs = (
        P(None, "gx", "gy", "gz"),
        P(None, "gx", "gy", "gz"),
        P("gx", "gy", "gz"),
        P("gx", "gy", "gz"),
        P("gx", "gy", "gz", None, None),
        P("gx", "gy", "gz", None, None),
    )
    out_specs = (P(None, "gx", "gy", "gz"), P(None, "gx", "gy", "gz"))
    return jax.shard_map(local, mesh=mesh, in_specs=in_specs, out_specs=out_specs, check_vma=False)
```
